32 devices in a mesh: gx: 8 (over y, x, core), gy: 4 (over z).
Axes of the slice: x: 2, y: 2, z: 4, core: 2. Of those that a mesh axis runs over, the one named last changes fastest.
Arguments:
- displacement: float32 [3, 128, 128, 128], P(None, 'gx', 'gy'), may hold values from -4 to 4
- force: float32 [3, 128, 128, 128], P(None, 'gx', 'gy'), may hold values from -12 to 12
- damage: float32 [128, 128, 128], P('gx', 'gy'), may hold values from 0 to 0.8
- history: float32 [128, 128, 128], P('gx', 'gy'), may hold values from 0.05 to 3
- crack_flags: int32 [128, 128, 128], P('gx', 'gy'), may hold values 0 or 1
Outputs:
- displacement_out: float32 [3, 128, 128, 128], P(None, 'gx', 'gy')
- damage_out: float32 [128, 128, 128], P('gx', 'gy')
- history_out: float32 [128, 128, 128], P('gx', 'gy')
The draws below stay inside these ranges and needn't reach their ends.
All inputs are finite; a program needn't handle non-finite values. No bound on the sum of `crack_flags` on one device may be relied on, other than what follows from the above.
Results may differ from the reference program's by a relative error of at most 0.0003.
Values sent between devices are 32-bit elements; how exact they have to be, the bound alone decides.
A program may use at most 64 MiB of HBM per device.

```python
import math
import jax
import jax.numpy as jnp

NZ = 128
ITERS = 3
NX = 128
NY = 128


def draw_force(key, part):
    key_rows = jax.random.fold_in(key, 11)
    key_values = jax.random.fold_in(key, 23)
    rising = 10.0 ** (0.5 * jnp.arange(NX, dtype=jnp.float32) / max(NX - 1, 1))
    across = 3.0 ** jax.random.uniform(key_rows, (NY,), jnp.float32, 0.0, 1.0)
    scales = 0.3 * rising[:, None, None] * across[None, :, None]
    values = jnp.clip(jax.random.normal(key_values, (3, NX, NY, NZ), jnp.float32), -4.0, 4.0)
    return values * scales[None]


def place_ends(values, stream_key, smallest, high):
    spot = [jax.random.randint(jax.random.fold_in(stream_key, axis), (), 0, length) for axis, length in enumerate(values.shape)]
    widest = values.shape.index(max(values.shape))
    beside = spot[:widest] + [(spot[widest] + 1) % values.shape[widest]] + spot[widest + 1:]
    return values.at[tuple(spot)].set(smallest).at[tuple(beside)].set(high)


def shard_levels(own_key, shape, pieces, low, largest):
    level, own = 1.0, jax.random.fold_in(own_key, 6)
    for dim, shards_of in pieces:
        steps = jnp.exp(jax.random.uniform(jax.random.fold_in(own, dim), (shards_of,), jnp.float32, low / len(pieces), largest / len(pieces)))
        level = level * jnp.repeat(steps, shape[dim] // shards_of).reshape([-1 if axis == dim else 1 for axis in range(len(shape))])
    return level


def noise(rng, dims, scale, limit, split=(), kind=jnp.bfloat16):
    values = scale * jax.random.normal(rng, dims, jnp.float32)
    if split:
        values = values * shard_levels(rng, dims, split, -0.22, 0.18)
    return jnp.clip(values, -limit, limit).astype(kind)


def setup_inputs(seed: int = 0) -> dict:
    arg_keys = jax.random.split(jax.random.key(seed), 6)
    return {
        "displacement": noise(arg_keys[0], (3, NX, NY, NZ), 0.3, 4.0, ((1, 8), (2, 4)), jnp.float32),
        "force": draw_force(jax.random.fold_in(arg_keys[5], 71), 0),
        "damage": jnp.clip(0.8 * jax.random.uniform(arg_keys[2], (NX, NY, NZ), jnp.float32) ** shard_levels(arg_keys[2], (NX, NY, NZ), ((0, 8), (1, 4)), -0.2, 0.2), 0.0, 0.8),
        "history": jnp.clip(jnp.exp(math.log(3.0) - 4.0943445 * jax.random.uniform(arg_keys[3], (NX, NY, NZ), jnp.float32) ** shard_levels(arg_keys[3], (NX, NY, NZ), ((0, 8), (1, 4)), -0.2, 0.2)), 0.05, 3.0),
        "crack_flags": place_ends((jax.random.randint(arg_keys[4], (NX, NY, NZ), 0, 16) < 1).astype(jnp.int32), jax.random.fold_in(arg_keys[4], 1), 0, 1),
    }


shear_modulus = 1.0
lame_first = 1.5
spring_term = 0.5
stiff_floor = 1e-3
crack_load = 4.0
tough_ratio = 0.5
length_term = 2.0
stress_index = ((0, 3, 4), (3, 1, 5), (4, 5, 2))


def strains(padded):
    base = padded[:, :-1, :-1, :-1]
    grads = []
    for component in range(3):
        grads.append((padded[component, 1:, :-1, :-1] - base[component],
                      padded[component, :-1, 1:, :-1] - base[component],
                      padded[component, :-1, :-1, 1:] - base[component]))
    return (grads[0][0], grads[1][1], grads[2][2],
            0.5 * (grads[0][1] + grads[1][0]),
            0.5 * (grads[0][2] + grads[2][0]),
            0.5 * (grads[1][2] + grads[2][1]))


def lowered(values, direction):
    if direction == 0:
        return values[:-1, 1:, 1:]
    if direction == 1:
        return values[1:, :-1, 1:]
    return values[1:, 1:, :-1]


def elastic(padded, padded_gain):
    strain = strains(padded)
    weight = padded_gain[:-1, :-1, :-1]
    trace = strain[0] + strain[1] + strain[2]
    stress = [weight * (2.0 * shear_modulus * strain[index] + lame_first * trace) for index in range(3)]
    stress = stress + [weight * (2.0 * shear_modulus * strain[index]) for index in range(3, 6)]
    images = []
    for component in range(3):
        summed = spring_term * padded[component, 1:-1, 1:-1, 1:-1]
        for direction in range(3):
            values = stress[stress_index[component][direction]]
            summed = summed + lowered(values, direction) - values[1:, 1:, 1:]
        images.append(summed)
    return jnp.stack(images), strain


def energy(strain):
    owned = [item[1:, 1:, 1:] for item in strain]
    trace = owned[0] + owned[1] + owned[2]
    squares = owned[0] ** 2 + owned[1] ** 2 + owned[2] ** 2 + 2.0 * (owned[3] ** 2 + owned[4] ** 2 + owned[5] ** 2)
    bulk_half = 0.5 * (lame_first + 2.0 * shear_modulus / 3.0)
    return bulk_half * jnp.maximum(trace, 0.0) ** 2 + shear_modulus * (squares - trace * trace / 3.0)


def damage_apply(padded, driving):
    center = padded[1:-1, 1:-1, 1:-1]
    beside_all = (padded[2:, 1:-1, 1:-1] + padded[:-2, 1:-1, 1:-1] + padded[1:-1, 2:, 1:-1]
              + padded[1:-1, :-2, 1:-1] + padded[1:-1, 1:-1, 2:] + padded[1:-1, 1:-1, :-2])
    return (tough_ratio + 2.0 * driving) * center + length_term * (6.0 * center - beside_all)


def pad_vector(values):
    return jnp.pad(values, ((0, 0), (1, 1), (1, 1), (1, 1)))


def conjugate(operate, start, target):
    current = start
    resid = target - operate(start)
    direction = resid
    norm_now = jnp.sum(resid * resid)
    for number in range(ITERS):
        image = operate(direction)
        alpha = norm_now / jnp.sum(direction * image)
        current = current + alpha * direction
        resid = resid - alpha * image
        norm_next = jnp.sum(resid * resid)
        direction = resid + (norm_next / norm_now) * direction
        norm_now = norm_next
    return current


def reference(displacement, force, damage, history, crack_flags):
    gain = (1.0 - damage) ** 2 + stiff_floor
    padded_gain = jnp.pad(gain, 1)

    def elastic_only(values):
        return elastic(pad_vector(values), padded_gain)[0]

    moved = conjugate(elastic_only, displacement, force)
    psi = energy(elastic(pad_vector(moved), padded_gain)[1])
    history_out = jnp.maximum(jnp.maximum(history, psi), crack_load * crack_flags.astype(jnp.float32))

    def damage_only(values):
        return damage_apply(jnp.pad(values, 1), history_out)

    damage_out = conjugate(damage_only, damage, 2.0 * history_out)
    return moved, damage_out, history_out
```

```python
import functools
import jax
import jax.numpy as jnp
from jax import lax
from jax.experimental import pallas as pl
from jax.experimental.pallas import tpu as pltpu
from jax.sharding import PartitionSpec as P

XO = 2
XF = 3
RO = 8
DIRS = ((1, 0), (-1, 0), (0, 1), (0, -1), (1, 1), (1, -1), (-1, 1), (-1, -1))
MESH = pl.DeviceIdType.MESH
U_EX, D_EX, R_EX, W_EX, H_EX = range(5)
WIDTHS = {
    U_EX: (3, 1, 1, 1, 1),
    D_EX: (1, 2, 2, 2, 2),
    R_EX: (3, 2, 3, 2, 4),
    W_EX: (1, 2, 3, 2, 4),
    H_EX: (1, 1, 2, 1, 2),
}


def galerkin(total):
    m = [total[k : k + 1, :] for k in range(6)]
    l10, l20 = m[2] / m[1], m[3] / m[1]
    d1 = m[3] - l10 * m[2]
    e1 = m[4] - l20 * m[2]
    l21 = e1 / d1
    f1 = m[5] - l20 * m[3] - l21 * e1
    z1 = m[1] - l10 * m[0]
    z2 = m[2] - l20 * m[0] - l21 * z1
    y2 = jnp.where(f1 > 0.0, z2 / f1, 0.0)
    y1 = jnp.where(d1 > 0.0, z1 / d1 - l21 * y2, 0.0)
    y2 = jnp.where(d1 > 0.0, y2, 0.0)
    y0 = m[0] / m[1] - l10 * y1 - l20 * y2
    y0 = jnp.where(d1 > 0.0, y0, m[0] / m[1])
    return y0, y1, y2


def kernel(sizes, u_in, f_in, d_in, hist_in, crack_in, u_out, d_out, h_out, *scratch):
    n_gx, n_gy, X, Y, Z = sizes
    (U, V0, V1, V2, S, G, D, H, W0, W1, W2, F, HI, CR) = scratch[:14]
    stages = scratch[14:34]
    part, gath, send_sem, recv_sem, ar_send, ar_recv, loc_sem = scratch[34:]
    n = n_gx * n_gy
    gx, gy = lax.axis_index("gx"), lax.axis_index("gy")
    me = gx * n_gy + gy
    own_x, own_y = pl.ds(XO, X), pl.ds(RO, Y)

    loads = (
        pltpu.make_async_copy(u_in, U.at[:, own_x, own_y], loc_sem.at[0]),
        pltpu.make_async_copy(d_in, D.at[0, own_x, own_y], loc_sem.at[1]),
        pltpu.make_async_copy(f_in, F, loc_sem.at[2]),
        pltpu.make_async_copy(hist_in, HI, loc_sem.at[3]),
        pltpu.make_async_copy(crack_in, CR, loc_sem.at[4]),
    )
    for item in loads:
        item.start()

    def peer(i):
        t = lax.rem(me + i, n)
        return (t // n_gy, lax.rem(t, n_gy))

    barrier = pltpu.get_barrier_semaphore()

    def greet(i, c):
        pl.semaphore_signal(barrier, inc=1, device_id=peer(i), device_id_type=MESH)
        return c

    lax.fori_loop(1, n, greet, 0)

    def exists(dx, dy):
        ok = None
        for pos, size, d in ((gx, n_gx, dx), (gy, n_gy, dy)):
            if d:
                one = (pos + d < size) if d > 0 else (pos + d >= 0)
                ok = one if ok is None else jnp.logical_and(ok, one)
        return ok

    def copy_of(number, buf, k):
        comps, xb, xf, rb, rf = WIDTHS[number]
        send_b, send_f, got_b, got_f = stages[4 * number : 4 * number + 4]
        dx, dy = DIRS[k]
        sx = {1: pl.ds(XO + X - xb, xb), -1: pl.ds(XO, xf), 0: own_x}[dx]
        tx = {1: pl.ds(XO - xb, xb), -1: pl.ds(XO + X, xf), 0: own_x}[dx]
        if dy == 0:
            src, dst = buf.at[:, sx, own_y], buf.at[:, tx, own_y]
        elif dy > 0:
            src, dst = send_b.at[:, sx], got_b.at[:, tx]
        else:
            src, dst = send_f.at[:, sx], got_f.at[:, tx]
        return pltpu.make_async_remote_copy(
            src_ref=src,
            dst_ref=dst,
            send_sem=send_sem.at[number, k],
            recv_sem=recv_sem.at[number, k],
            device_id=(gx + dx, gy + dy),
            device_id_type=MESH,
        )

    def send(number, buf):
        comps, xb, xf, rb, rf = WIDTHS[number]
        send_b, send_f = stages[4 * number : 4 * number + 2]

        def go(k):
            pl.when(exists(*DIRS[k]))(lambda: copy_of(number, buf, k).start())

        go(0)
        go(1)

        def pack(x, c):
            for comp in range(comps):
                send_b[comp, x] = buf[comp, x, RO + Y - rb : RO + Y, :]
                send_f[comp, x] = buf[comp, x, RO : RO + rf, :]
            return c

        lax.fori_loop(XO, XO + X, pack, 0, unroll=2)
        for k in range(2, 8):
            go(k)

    def receive(number, buf):
        comps, xb, xf, rb, rf = WIDTHS[number]
        got_b, got_f = stages[4 * number + 2 : 4 * number + 4]
        for k in range(8):
            dx, dy = DIRS[k]
            pl.when(exists(-dx, -dy))(lambda k=k: copy_of(number, buf, k).wait_recv())
        has_b, has_f = gy > 0, gy + 1 < n_gy

        def unpack(x, c):
            for comp in range(comps):
                buf[comp, x, RO - rb : RO, :] = jnp.where(has_b, got_b[comp, x], 0.0)
                buf[comp, x, RO + Y : RO + Y + rf, :] = jnp.where(has_f, got_f[comp, x], 0.0)
            return c

        lax.fori_loop(XO - xb, XO + X + xf, unpack, 0)
        rows = buf.shape[2]

        @pl.when(gx == 0)
        def _():
            buf[:, XO - xb : XO] = jnp.zeros((comps, xb, rows, Z), jnp.float32)

        @pl.when(gx == n_gx - 1)
        def _():
            buf[:, XO + X : XO + X + xf] = jnp.zeros((comps, xf, rows, Z), jnp.float32)

    def sent(number, buf):
        for k in range(8):
            pl.when(exists(*DIRS[k]))(lambda k=k: copy_of(number, buf, k).wait_send())

    def lanes(rows):
        return lax.broadcasted_iota(jnp.int32, (rows, Z), 1)

    def next_z(a):
        return jnp.where(lanes(a.shape[0]) == Z - 1, 0.0, pltpu.roll(a, Z - 1, 1))

    def last_z(a):
        return jnp.where(lanes(a.shape[0]) == 0, 0.0, pltpu.roll(a, 1, 1))

    def inside(x, r0, rows):
        at = lax.broadcasted_iota(jnp.int32, (rows, Z), 0) + (gy * Y + (r0 - RO))
        xg = gx * X + (x - XO)
        top = jnp.where(jnp.logical_and(xg >= 0, xg < n_gx * X), n_gy * Y, 0)
        return jnp.logical_and(at >= 0, at < top)

    def grads(src, x, r0, rows):
        here = [src[c, x, r0 : r0 + rows, :] for c in range(3)]
        result = []
        for c in range(3):
            result.append(
                (
                    src[c, x + 1, r0 : r0 + rows, :] - here[c],
                    src[c, x, r0 + 1 : r0 + 1 + rows, :] - here[c],
                    next_z(here[c]) - here[c],
                )
            )
        return here, result

    def stress(src, x, r0, rows):
        here, d = grads(src, x, r0, rows)
        g = G[x, r0 : r0 + rows, :]
        g2 = g + g
        lam = (1.5 * g) * (d[0][0] + d[1][1] + d[2][2])
        S[0, x, r0 : r0 + rows, :] = g2 * d[0][0] + lam
        S[1, x, r0 : r0 + rows, :] = g2 * d[1][1] + lam
        S[2, x, r0 : r0 + rows, :] = g2 * d[2][2] + lam
        S[3, x, r0 : r0 + rows, :] = g * (d[0][1] + d[1][0])
        S[4, x, r0 : r0 + rows, :] = g * (d[0][2] + d[2][0])
        S[5, x, r0 : r0 + rows, :] = g * (d[1][2] + d[2][1])

    index = ((0, 3, 4), (3, 1, 5), (4, 5, 2))

    def divergence(src, x, r0, rows):
        at = [S[k, x, r0 : r0 + rows, :] for k in range(6)]
        images = []
        for c in range(3):
            ix, iy, iz = index[c]
            total = 0.5 * src[c, x, r0 : r0 + rows, :]
            total = total + (S[ix, x - 1, r0 : r0 + rows, :] - at[ix])
            total = total + (S[iy, x, r0 - 1 : r0 - 1 + rows, :] - at[iy])
            total = total + (last_z(at[iz]) - at[iz])
            images.append(total)
        return images

    def apply_elastic(src, dst, x0, x1, r0, rows, s_rows):
        stress(src, x0 - 1, r0 - 1, s_rows)

        def step(x, c):
            stress(src, x, r0 - 1, s_rows)
            images = divergence(src, x, r0, rows)
            if dst is V0:
                for comp in range(3):
                    V0[comp, x, r0 : r0 + rows, :] = F[comp, x - XO] - images[comp]
            else:
                ok = inside(x, r0, rows)
                for comp in range(3):
                    dst[comp, x, r0 : r0 + rows, :] = jnp.where(ok, images[comp], 0.0)
            return c

        lax.fori_loop(x0, x1, step, 0)

    def fold(a):
        total = a[0:8]
        for k in range(1, a.shape[0] // 8):
            total = total + a[8 * k : 8 * k + 8]
        return total

    def all_sum(number, accs):
        lane = lax.broadcasted_iota(jnp.int32, (1, Z), 1)
        row = jnp.zeros((1, Z), jnp.float32)
        for k, a in enumerate(accs):
            one = jnp.sum(jnp.sum(a, axis=0, keepdims=True), axis=1, keepdims=True)
            row = jnp.where(lane == k, one, row)
        part[number, 0] = row
        gath[number, me] = row

        def go(i, c):
            pltpu.make_async_remote_copy(
                src_ref=part.at[number, 0],
                dst_ref=gath.at[number, me],
                send_sem=ar_send.at[number],
                recv_sem=ar_recv.at[number],
                device_id=peer(i),
                device_id_type=MESH,
            ).start()
            return c

        lax.fori_loop(1, n, go, 0)

    def all_wait(number):
        whole = gath.at[number, pl.ds(0, n - 1)]
        pltpu.make_async_copy(whole, whole, ar_recv.at[number]).wait()
        pltpu.make_async_copy(whole, whole, ar_send.at[number]).wait()
        row = jnp.sum(gath[number], axis=0)
        wide = jnp.broadcast_to(row, (8, Z))
        diag = lax.broadcasted_iota(jnp.int32, (8, Z), 0) == lanes(8)
        column = jnp.sum(jnp.where(diag, wide, 0.0), axis=1, keepdims=True)
        return galerkin(jnp.broadcast_to(column, (8, Z)))

    loads[0].wait()
    loads[1].wait()
    pl.semaphore_wait(barrier, n - 1)
    send(U_EX, U)
    send(D_EX, D)
    receive(D_EX, D)
    all_rows = RO + Y + RO

    def make_gain(x, c):
        left = 1.0 - D[0, x]
        G[x] = jnp.where(inside(x, 0, all_rows), left * left + 0.001, 0.0)
        return c

    lax.fori_loop(XO - 2, XO + X + 2, make_gain, 0)
    loads[2].wait()
    receive(U_EX, U)
    apply_elastic(U, V0, XO, XO + X, RO, Y, Y + 8)
    send(R_EX, V0)
    loads[3].wait()
    loads[4].wait()
    receive(R_EX, V0)
    apply_elastic(V0, V1, XO - 1, XO + X + 2, RO - 1, Y + 8, Y + 8)
    apply_elastic(V1, V2, XO, XO + X + 1, RO - 1, Y + 8, Y + 8)

    def moments(x, accs):
        here, d = grads(V2, x, RO, Y)
        g = G[x, RO : RO + Y, :]
        tr = d[0][0] + d[1][1] + d[2][2]
        s01, s02, s12 = d[0][1] + d[1][0], d[0][2] + d[2][0], d[1][2] + d[2][1]
        normal = d[0][0] * d[0][0] + d[1][1] * d[1][1] + d[2][2] * d[2][2]
        energy = g * (2.0 * normal + (s01 * s01 + s02 * s02 + s12 * s12) + 1.5 * tr * tr)
        v0 = [V0[c, x, RO : RO + Y, :] for c in range(3)]
        v1 = [V1[c, x, RO : RO + Y, :] for c in range(3)]

        def dot(a, b):
            return a[0] * b[0] + a[1] * b[1] + a[2] * b[2]

        m4 = dot(here, here)
        terms = (dot(v0, v0), dot(v0, v1), dot(v1, v1), dot(v1, here), m4, energy + 0.5 * m4)
        return tuple(acc + fold(term) for acc, term in zip(accs, terms))

    zero = tuple(jnp.zeros((8, Z), jnp.float32) for _ in range(6))
    all_sum(0, lax.fori_loop(XO, XO + X, moments, zero))
    sent(U_EX, U)
    sent(R_EX, V0)
    sent(D_EX, D)
    y0, y1, y2 = all_wait(0)

    def move(x, c):
        for comp in range(3):
            rows = pl.ds(RO, Y + 8)
            U[comp, x, rows, :] = (
                U[comp, x, rows, :]
                + y0 * V0[comp, x, rows, :]
                + y1 * V1[comp, x, rows, :]
                + y2 * V2[comp, x, rows, :]
            )
        return c

    lax.fori_loop(XO, XO + X + 1, move, 0)
    u_store = pltpu.make_async_copy(U.at[:, own_x, own_y], u_out, loc_sem.at[5])
    u_store.start()

    def beside(src, x, r0, rows):
        here = src[0, x, r0 : r0 + rows, :]
        ahead = src[0, x + 1, r0 : r0 + rows, :] + src[0, x, r0 + 1 : r0 + 1 + rows, :] + next_z(here)
        behind = src[0, x - 1, r0 : r0 + rows, :] + src[0, x, r0 - 1 : r0 - 1 + rows, :] + last_z(here)
        return here, ahead, behind

    def drive(x, c):
        here, d = grads(U, x, RO, Y)
        tr = d[0][0] + d[1][1] + d[2][2]
        s01, s02, s12 = d[0][1] + d[1][0], d[0][2] + d[2][0], d[1][2] + d[2][1]
        squares = d[0][0] * d[0][0] + d[1][1] * d[1][1] + d[2][2] * d[2][2]
        squares = squares + 0.5 * (s01 * s01 + s02 * s02 + s12 * s12)
        up = jnp.maximum(tr, 0.0)
        psi = (0.5 * (1.5 + 2.0 / 3.0)) * up * up + (squares - tr * tr * (1.0 / 3.0))
        flags = 4.0 * CR[x - XO].astype(jnp.float32)
        h = jnp.maximum(jnp.maximum(HI[x - XO], psi), flags)
        H[0, x, RO : RO + Y, :] = h
        now, ahead, behind = beside(D, x, RO, Y)
        image = (0.5 + 2.0 * h) * now + 2.0 * (6.0 * now - (ahead + behind))
        W0[0, x, RO : RO + Y, :] = 2.0 * h - image
        return c

    lax.fori_loop(XO, XO + X, drive, 0)
    send(W_EX, W0)
    send(H_EX, H)
    h_store = pltpu.make_async_copy(H.at[0, own_x, own_y], h_out, loc_sem.at[6])
    h_store.start()
    receive(W_EX, W0)
    receive(H_EX, H)

    def apply_damage(src, dst, x0, x1):
        r0, rows = RO - 1, Y + 8

        def step(x, c):
            here, ahead, behind = beside(src, x, r0, rows)
            h = H[0, x, r0 : r0 + rows, :]
            image = (0.5 + 2.0 * h) * here + 2.0 * (6.0 * here - (ahead + behind))
            dst[0, x, r0 : r0 + rows, :] = jnp.where(inside(x, r0, rows), image, 0.0)
            return c

        lax.fori_loop(x0, x1, step, 0)

    apply_damage(W0, W1, XO - 1, XO + X + 2)
    apply_damage(W1, W2, XO, XO + X + 1)

    def damage_moments(x, accs):
        w2 = W2[0, x, RO : RO + Y, :]
        ahead = W2[0, x + 1, RO : RO + Y, :] + W2[0, x, RO + 1 : RO + 1 + Y, :] + next_z(w2)
        w0, w1 = W0[0, x, RO : RO + Y, :], W1[0, x, RO : RO + Y, :]
        m5 = w2 * ((12.5 + 2.0 * H[0, x, RO : RO + Y, :]) * w2 - 4.0 * ahead)
        terms = (w0 * w0, w0 * w1, w1 * w1, w1 * w2, w2 * w2, m5)
        return tuple(acc + fold(term) for acc, term in zip(accs, terms))

    all_sum(1, lax.fori_loop(XO, XO + X, damage_moments, zero))
    sent(W_EX, W0)
    sent(H_EX, H)
    y0, y1, y2 = all_wait(1)

    def heal(x, c):
        rows = pl.ds(RO, Y)
        D[0, x, rows, :] = (
            D[0, x, rows, :]
            + y0 * W0[0, x, rows, :]
            + y1 * W1[0, x, rows, :]
            + y2 * W2[0, x, rows, :]
        )
        return c

    lax.fori_loop(XO, XO + X, heal, 0)
    d_store = pltpu.make_async_copy(D.at[0, own_x, own_y], d_out, loc_sem.at[7])
    d_store.start()
    u_store.wait()
    h_store.wait()
    d_store.wait()


def body(n_gx, n_gy, displacement, force, damage, history, crack_flags):
    _, X, Y, Z = displacement.shape
    slabs, rows = XO + X + XF, RO + Y + RO
    n = n_gx * n_gy
    f32 = jnp.float32

    def field(comps):
        return pltpu.VMEM((comps, slabs, rows, Z), f32)

    scratch = [field(3)] * 4 + [field(6), pltpu.VMEM((slabs, rows, Z), f32)]
    scratch += [field(1)] * 5
    scratch += [
        pltpu.VMEM((3, X, Y, Z), f32),
        pltpu.VMEM((X, Y, Z), f32),
        pltpu.VMEM((X, Y, Z), crack_flags.dtype),
    ]
    for number in range(5):
        comps, xb, xf, rb, rf = WIDTHS[number]
        scratch += [pltpu.VMEM((comps, slabs, r, Z), f32) for r in (rb, rf, rb, rf)]
    scratch += [
        pltpu.VMEM((2, 1, 1, Z), f32),
        pltpu.VMEM((2, n, 1, Z), f32),
        pltpu.SemaphoreType.DMA((5, 8)),
        pltpu.SemaphoreType.DMA((5, 8)),
        pltpu.SemaphoreType.DMA((2,)),
        pltpu.SemaphoreType.DMA((2,)),
        pltpu.SemaphoreType.DMA((8,)),
    ]
    scalar = jax.ShapeDtypeStruct((X, Y, Z), f32)
    return pl.pallas_call(
        functools.partial(kernel, (n_gx, n_gy, X, Y, Z)),
        out_shape=(jax.ShapeDtypeStruct(displacement.shape, f32), scalar, scalar),
        in_specs=[pl.BlockSpec(memory_space=pl.ANY)] * 5,
        out_specs=tuple([pl.BlockSpec(memory_space=pl.ANY)] * 3),
        scratch_shapes=scratch,
        compiler_params=pltpu.CompilerParams(
            collective_id=0, has_side_effects=True, vmem_limit_bytes=48 * 1024 * 1024
        ),
    )(displacement, force, damage, history, crack_flags)


def solution(mesh):
    return jax.shard_map(
        functools.partial(body, mesh.shape["gx"], mesh.shape["gy"]),
        mesh=mesh,
        in_specs=(
            P(None, "gx", "gy", None),
            P(None, "gx", "gy", None),
            P("gx", "gy", None),
            P("gx", "gy", None),
            P("gx", "gy", None),
        ),
        out_specs=(P(None, "gx", "gy", None), P("gx", "gy", None), P("gx", "gy", None)),
        check_vma=False,
    )
```

```python
import functools
import jax
import jax.numpy as jnp
from jax import lax
from jax.experimental import pallas as pl
from jax.experimental.pallas import tpu as pltpu
from jax.sharding import PartitionSpec as P

UNROLL = 4
SHIFT_U = 8.0
SHIFT_D = 15.0
XO = 2
XF = 3
RO = 8
DIRS = ((1, 0), (-1, 0), (0, 1), (0, -1), (1, 1), (1, -1), (-1, 1), (-1, -1))
MESH = pl.DeviceIdType.MESH
U_EX, D_EX, R_EX, W_EX, H_EX = range(5)
WIDTHS = {
    U_EX: (3, 1, 1, 1, 1),
    D_EX: (1, 2, 2, 2, 2),
    R_EX: (3, 2, 3, 2, 4),
    W_EX: (1, 2, 3, 2, 4),
    H_EX: (1, 1, 2, 1, 2),
}


def galerkin(total, shift):
    g00, g01, g02, g11, g12, g22, h22 = [total[k : k + 1, :] for k in range(7)]
    h00, h01, h02 = g01 + shift * g00, g11 + shift * g01, g12 + shift * g02
    h11, h12 = g12 + shift * g11, g22 + shift * g12
    l10, l20 = h01 / h00, h02 / h00
    d1 = h11 - l10 * h01
    e1 = h12 - l20 * h01
    l21 = e1 / d1
    f1 = h22 - l20 * h02 - l21 * e1
    z1 = g01 - l10 * g00
    z2 = g02 - l20 * g00 - l21 * z1
    y2 = jnp.where(f1 > 0.0, z2 / f1, 0.0)
    y1 = jnp.where(d1 > 0.0, z1 / d1 - l21 * y2, 0.0)
    y2 = jnp.where(d1 > 0.0, y2, 0.0)
    y0 = g00 / h00 - l10 * y1 - l20 * y2
    y0 = jnp.where(d1 > 0.0, y0, g00 / h00)
    return y0, y1, y2


def kernel(sizes, u_in, f_in, d_in, hist_in, crack_in, u_out, d_out, h_out, *scratch):
    n_gx, n_gy, X, Y, Z = sizes
    (U, V0, V1, V2, S, G, D, H, W0, W1, W2, F, HI, CR) = scratch[:14]
    stages = scratch[14:34]
    part, gath, send_sem, recv_sem, ar_send, ar_recv, loc_sem = scratch[34:]
    n = n_gx * n_gy
    gx, gy = lax.axis_index("gx"), lax.axis_index("gy")
    me = gx * n_gy + gy
    own_x, own_y = pl.ds(XO, X), pl.ds(RO, Y)

    loads = (
        pltpu.make_async_copy(u_in, U.at[:, own_x, own_y], loc_sem.at[0]),
        pltpu.make_async_copy(d_in, D.at[0, own_x, own_y], loc_sem.at[1]),
        pltpu.make_async_copy(f_in, F, loc_sem.at[2]),
        pltpu.make_async_copy(hist_in, HI, loc_sem.at[3]),
        pltpu.make_async_copy(crack_in, CR, loc_sem.at[4]),
    )
    for item in loads:
        item.start()

    def peer(i):
        t = lax.rem(me + i, n)
        return (t // n_gy, lax.rem(t, n_gy))

    barrier = pltpu.get_barrier_semaphore()

    def greet(i, c):
        pl.semaphore_signal(barrier, inc=1, device_id=peer(i), device_id_type=MESH)
        return c

    lax.fori_loop(1, n, greet, 0)

    def exists(dx, dy):
        ok = None
        for pos, size, d in ((gx, n_gx, dx), (gy, n_gy, dy)):
            if d:
                one = (pos + d < size) if d > 0 else (pos + d >= 0)
                ok = one if ok is None else jnp.logical_and(ok, one)
        return ok

    def copy_of(number, buf, k):
        comps, xb, xf, rb, rf = WIDTHS[number]
        send_b, send_f, got_b, got_f = stages[4 * number : 4 * number + 4]
        dx, dy = DIRS[k]
        sx = {1: pl.ds(XO + X - xb, xb), -1: pl.ds(XO, xf), 0: own_x}[dx]
        tx = {1: pl.ds(XO - xb, xb), -1: pl.ds(XO + X, xf), 0: own_x}[dx]
        if dy == 0:
            src, dst = buf.at[:, sx, own_y], buf.at[:, tx, own_y]
        elif dy > 0:
            src, dst = send_b.at[:, sx], got_b.at[:, tx]
        else:
            src, dst = send_f.at[:, sx], got_f.at[:, tx]
        return pltpu.make_async_remote_copy(
            src_ref=src,
            dst_ref=dst,
            send_sem=send_sem.at[number, k],
            recv_sem=recv_sem.at[number, k],
            device_id=(gx + dx, gy + dy),
            device_id_type=MESH,
        )

    def send(number, buf):
        comps, xb, xf, rb, rf = WIDTHS[number]
        send_b, send_f = stages[4 * number : 4 * number + 2]

        def go(k):
            pl.when(exists(*DIRS[k]))(lambda: copy_of(number, buf, k).start())

        go(0)
        go(1)

        def pack(x, c):
            for comp in range(comps):
                send_b[comp, x] = buf[comp, x, RO + Y - rb : RO + Y, :]
                send_f[comp, x] = buf[comp, x, RO : RO + rf, :]
            return c

        lax.fori_loop(XO, XO + X, pack, 0, unroll=UNROLL)
        for k in range(2, 8):
            go(k)

    def receive(number, buf):
        comps, xb, xf, rb, rf = WIDTHS[number]
        got_b, got_f = stages[4 * number + 2 : 4 * number + 4]
        for k in range(8):
            dx, dy = DIRS[k]
            pl.when(exists(-dx, -dy))(lambda k=k: copy_of(number, buf, k).wait_recv())
        has_b, has_f = gy > 0, gy + 1 < n_gy

        def unpack(x, c):
            for comp in range(comps):
                buf[comp, x, RO - rb : RO, :] = jnp.where(has_b, got_b[comp, x], 0.0)
                buf[comp, x, RO + Y : RO + Y + rf, :] = jnp.where(has_f, got_f[comp, x], 0.0)
            return c

        lax.fori_loop(XO - xb, XO + X + xf, unpack, 0, unroll=UNROLL)
        rows = buf.shape[2]

        @pl.when(gx == 0)
        def _():
            buf[:, XO - xb : XO] = jnp.zeros((comps, xb, rows, Z), jnp.float32)

        @pl.when(gx == n_gx - 1)
        def _():
            buf[:, XO + X : XO + X + xf] = jnp.zeros((comps, xf, rows, Z), jnp.float32)

    def sent(number, buf):
        for k in range(8):
            pl.when(exists(*DIRS[k]))(lambda k=k: copy_of(number, buf, k).wait_send())

    def lanes(rows):
        return lax.broadcasted_iota(jnp.int32, (rows, Z), 1)

    def next_z(a):
        return jnp.where(lanes(a.shape[0]) == Z - 1, 0.0, pltpu.roll(a, Z - 1, 1))

    def last_z(a):
        return jnp.where(lanes(a.shape[0]) == 0, 0.0, pltpu.roll(a, 1, 1))

    def inside(x, r0, rows):
        at = lax.broadcasted_iota(jnp.int32, (rows, Z), 0) + (gy * Y + (r0 - RO))
        xg = gx * X + (x - XO)
        top = jnp.where(jnp.logical_and(xg >= 0, xg < n_gx * X), n_gy * Y, 0)
        return jnp.logical_and(at >= 0, at < top)

    def grads(src, x, r0, rows):
        here = [src[c, x, r0 : r0 + rows, :] for c in range(3)]
        result = []
        for c in range(3):
            result.append(
                (
                    src[c, x + 1, r0 : r0 + rows, :] - here[c],
                    src[c, x, r0 + 1 : r0 + 1 + rows, :] - here[c],
                    next_z(here[c]) - here[c],
                )
            )
        return here, result

    def stress(src, x, r0, rows):
        here, d = grads(src, x, r0, rows)
        g = G[x, r0 : r0 + rows, :]
        g2 = g + g
        lam = (1.5 * g) * (d[0][0] + d[1][1] + d[2][2])
        S[0, x, r0 : r0 + rows, :] = g2 * d[0][0] + lam
        S[1, x, r0 : r0 + rows, :] = g2 * d[1][1] + lam
        S[2, x, r0 : r0 + rows, :] = g2 * d[2][2] + lam
        S[3, x, r0 : r0 + rows, :] = g * (d[0][1] + d[1][0])
        S[4, x, r0 : r0 + rows, :] = g * (d[0][2] + d[2][0])
        S[5, x, r0 : r0 + rows, :] = g * (d[1][2] + d[2][1])

    index = ((0, 3, 4), (3, 1, 5), (4, 5, 2))

    def divergence(src, x, r0, rows, spring):
        at = [S[k, x, r0 : r0 + rows, :] for k in range(6)]
        images = []
        for c in range(3):
            ix, iy, iz = index[c]
            total = spring * src[c, x, r0 : r0 + rows, :]
            total = total + (S[ix, x - 1, r0 : r0 + rows, :] - at[ix])
            total = total + (S[iy, x, r0 - 1 : r0 - 1 + rows, :] - at[iy])
            total = total + (last_z(at[iz]) - at[iz])
            images.append(total)
        return images

    def apply_elastic(src, dst, x0, x1, r0, rows, s_rows):
        spring = 0.5 if dst is V0 else 0.5 - SHIFT_U

        def strain_step(x, c):
            stress(src, x, r0 - 1, s_rows)
            return c

        lax.fori_loop(x0 - 1, x1, strain_step, 0, unroll=UNROLL)

        def step(x, c):
            images = divergence(src, x, r0, rows, spring)
            if dst is V0:
                for comp in range(3):
                    V0[comp, x, r0 : r0 + rows, :] = F[comp, x - XO] - images[comp]
            else:
                ok = inside(x, r0, rows)
                for comp in range(3):
                    dst[comp, x, r0 : r0 + rows, :] = jnp.where(ok, images[comp], 0.0)
            return c

        lax.fori_loop(x0, x1, step, 0, unroll=UNROLL)

    def fold(a):
        total = a[0:8]
        for k in range(1, a.shape[0] // 8):
            total = total + a[8 * k : 8 * k + 8]
        return total

    def all_sum(number, accs):
        lane = lax.broadcasted_iota(jnp.int32, (1, Z), 1)
        row = jnp.zeros((1, Z), jnp.float32)
        for k, a in enumerate(accs):
            one = jnp.sum(jnp.sum(a, axis=0, keepdims=True), axis=1, keepdims=True)
            row = jnp.where(lane == k, one, row)
        part[number, 0] = row
        gath[number, me] = row

        def go(i, c):
            pltpu.make_async_remote_copy(
                src_ref=part.at[number, 0],
                dst_ref=gath.at[number, me],
                send_sem=ar_send.at[number],
                recv_sem=ar_recv.at[number],
                device_id=peer(i),
                device_id_type=MESH,
            ).start()
            return c

        lax.fori_loop(1, n, go, 0)

    def all_wait(number, shift):
        whole = gath.at[number, pl.ds(0, n - 1)]
        pltpu.make_async_copy(whole, whole, ar_recv.at[number]).wait()
        pltpu.make_async_copy(whole, whole, ar_send.at[number]).wait()
        row = jnp.sum(gath[number], axis=0)
        wide = jnp.broadcast_to(row, (8, Z))
        diag = lax.broadcasted_iota(jnp.int32, (8, Z), 0) == lanes(8)
        column = jnp.sum(jnp.where(diag, wide, 0.0), axis=1, keepdims=True)
        return galerkin(jnp.broadcast_to(column, (8, Z)), shift)

    loads[0].wait()
    loads[1].wait()
    pl.semaphore_wait(barrier, n - 1)
    send(U_EX, U)
    send(D_EX, D)
    receive(D_EX, D)
    all_rows = RO + Y + RO

    def make_gain(x, c):
        left = 1.0 - D[0, x]
        G[x] = jnp.where(inside(x, 0, all_rows), left * left + 0.001, 0.0)
        return c

    lax.fori_loop(XO - 2, XO + X + 2, make_gain, 0, unroll=UNROLL)
    loads[2].wait()
    receive(U_EX, U)
    apply_elastic(U, V0, XO, XO + X, RO, Y, Y + 8)
    send(R_EX, V0)
    loads[3].wait()
    loads[4].wait()
    receive(R_EX, V0)
    apply_elastic(V0, V1, XO - 1, XO + X + 2, RO - 1, Y + 8, Y + 8)
    apply_elastic(V1, V2, XO, XO + X + 1, RO - 1, Y + 8, Y + 8)

    def moments(x, accs):
        here, d = grads(V2, x, RO, Y)
        g = G[x, RO : RO + Y, :]
        tr = d[0][0] + d[1][1] + d[2][2]
        s01, s02, s12 = d[0][1] + d[1][0], d[0][2] + d[2][0], d[1][2] + d[2][1]
        normal = d[0][0] * d[0][0] + d[1][1] * d[1][1] + d[2][2] * d[2][2]
        energy = g * (2.0 * normal + (s01 * s01 + s02 * s02 + s12 * s12) + 1.5 * tr * tr)
        v0 = [V0[c, x, RO : RO + Y, :] for c in range(3)]
        v1 = [V1[c, x, RO : RO + Y, :] for c in range(3)]

        def dot(a, b):
            return a[0] * b[0] + a[1] * b[1] + a[2] * b[2]

        m4 = dot(here, here)
        terms = (dot(v0, v0), dot(v0, v1), dot(v0, here), dot(v1, v1))
        terms = terms + (dot(v1, here), m4, energy + 0.5 * m4)
        return tuple(acc + fold(term) for acc, term in zip(accs, terms))

    zero = tuple(jnp.zeros((8, Z), jnp.float32) for _ in range(7))
    all_sum(0, lax.fori_loop(XO, XO + X, moments, zero, unroll=2))
    sent(U_EX, U)
    sent(R_EX, V0)
    sent(D_EX, D)
    y0, y1, y2 = all_wait(0, SHIFT_U)

    def move(x, c):
        for comp in range(3):
            rows = pl.ds(RO, Y + 8)
            U[comp, x, rows, :] = (
                U[comp, x, rows, :]
                + y0 * V0[comp, x, rows, :]
                + y1 * V1[comp, x, rows, :]
                + y2 * V2[comp, x, rows, :]
            )
        return c

    lax.fori_loop(XO, XO + X + 1, move, 0, unroll=2)
    u_store = pltpu.make_async_copy(U.at[:, own_x, own_y], u_out, loc_sem.at[5])
    u_store.start()

    def beside(src, x, r0, rows):
        here = src[0, x, r0 : r0 + rows, :]
        ahead = src[0, x + 1, r0 : r0 + rows, :] + src[0, x, r0 + 1 : r0 + 1 + rows, :] + next_z(here)
        behind = src[0, x - 1, r0 : r0 + rows, :] + src[0, x, r0 - 1 : r0 - 1 + rows, :] + last_z(here)
        return here, ahead, behind

    def drive(x, c):
        here, d = grads(U, x, RO, Y)
        tr = d[0][0] + d[1][1] + d[2][2]
        s01, s02, s12 = d[0][1] + d[1][0], d[0][2] + d[2][0], d[1][2] + d[2][1]
        squares = d[0][0] * d[0][0] + d[1][1] * d[1][1] + d[2][2] * d[2][2]
        squares = squares + 0.5 * (s01 * s01 + s02 * s02 + s12 * s12)
        up = jnp.maximum(tr, 0.0)
        psi = (0.5 * (1.5 + 2.0 / 3.0)) * up * up + (squares - tr * tr * (1.0 / 3.0))
        flags = 4.0 * CR[x - XO].astype(jnp.float32)
        h = jnp.maximum(jnp.maximum(HI[x - XO], psi), flags)
        H[0, x, RO : RO + Y, :] = h
        now, ahead, behind = beside(D, x, RO, Y)
        image = (0.5 + 2.0 * h) * now + 2.0 * (6.0 * now - (ahead + behind))
        W0[0, x, RO : RO + Y, :] = 2.0 * h - image
        return c

    lax.fori_loop(XO, XO + X, drive, 0, unroll=2)
    send(W_EX, W0)
    send(H_EX, H)
    h_store = pltpu.make_async_copy(H.at[0, own_x, own_y], h_out, loc_sem.at[6])
    h_store.start()
    receive(W_EX, W0)
    receive(H_EX, H)

    def apply_damage(src, dst, x0, x1):
        r0, rows = RO - 1, Y + 8

        def step(x, c):
            here, ahead, behind = beside(src, x, r0, rows)
            h = H[0, x, r0 : r0 + rows, :]
            image = ((12.5 - SHIFT_D) + 2.0 * h) * here - 2.0 * (ahead + behind)
            dst[0, x, r0 : r0 + rows, :] = jnp.where(inside(x, r0, rows), image, 0.0)
            return c

        lax.fori_loop(x0, x1, step, 0, unroll=UNROLL)

    apply_damage(W0, W1, XO - 1, XO + X + 2)
    apply_damage(W1, W2, XO, XO + X + 1)

    def damage_moments(x, accs):
        w2 = W2[0, x, RO : RO + Y, :]
        ahead = W2[0, x + 1, RO : RO + Y, :] + W2[0, x, RO + 1 : RO + 1 + Y, :] + next_z(w2)
        w0, w1 = W0[0, x, RO : RO + Y, :], W1[0, x, RO : RO + Y, :]
        m5 = w2 * ((12.5 + 2.0 * H[0, x, RO : RO + Y, :]) * w2 - 4.0 * ahead)
        terms = (w0 * w0, w0 * w1, w0 * w2, w1 * w1, w1 * w2, w2 * w2, m5)
        return tuple(acc + fold(term) for acc, term in zip(accs, terms))

    all_sum(1, lax.fori_loop(XO, XO + X, damage_moments, zero, unroll=2))
    sent(W_EX, W0)
    sent(H_EX, H)
    y0, y1, y2 = all_wait(1, SHIFT_D)

    def heal(x, c):
        rows = pl.ds(RO, Y)
        D[0, x, rows, :] = (
            D[0, x, rows, :]
            + y0 * W0[0, x, rows, :]
            + y1 * W1[0, x, rows, :]
            + y2 * W2[0, x, rows, :]
        )
        return c

    lax.fori_loop(XO, XO + X, heal, 0, unroll=UNROLL)
    d_store = pltpu.make_async_copy(D.at[0, own_x, own_y], d_out, loc_sem.at[7])
    d_store.start()
    u_store.wait()
    h_store.wait()
    d_store.wait()


def body(n_gx, n_gy, displacement, force, damage, history, crack_flags):
    _, X, Y, Z = displacement.shape
    slabs, rows = XO + X + XF, RO + Y + RO
    n = n_gx * n_gy
    f32 = jnp.float32

    def field(comps):
        return pltpu.VMEM((comps, slabs, rows, Z), f32)

    scratch = [field(3)] * 4 + [field(6), pltpu.VMEM((slabs, rows, Z), f32)]
    scratch += [field(1)] * 5
    scratch += [
        pltpu.VMEM((3, X, Y, Z), f32),
        pltpu.VMEM((X, Y, Z), f32),
        pltpu.VMEM((X, Y, Z), crack_flags.dtype),
    ]
    for number in range(5):
        comps, xb, xf, rb, rf = WIDTHS[number]
        scratch += [pltpu.VMEM((comps, slabs, r, Z), f32) for r in (rb, rf, rb, rf)]
    scratch += [
        pltpu.VMEM((2, 1, 1, Z), f32),
        pltpu.VMEM((2, n, 1, Z), f32),
        pltpu.SemaphoreType.DMA((5, 8)),
        pltpu.SemaphoreType.DMA((5, 8)),
        pltpu.SemaphoreType.DMA((2,)),
        pltpu.SemaphoreType.DMA((2,)),
        pltpu.SemaphoreType.DMA((8,)),
    ]
    scalar = jax.ShapeDtypeStruct((X, Y, Z), f32)
    return pl.pallas_call(
        functools.partial(kernel, (n_gx, n_gy, X, Y, Z)),
        out_shape=(jax.ShapeDtypeStruct(displacement.shape, f32), scalar, scalar),
        in_specs=[pl.BlockSpec(memory_space=pltpu.HBM)] * 5,
        out_specs=tuple([pl.BlockSpec(memory_space=pl.ANY)] * 3),
        scratch_shapes=scratch,
        compiler_params=pltpu.CompilerParams(
            collective_id=0, has_side_effects=True, vmem_limit_bytes=67043328
        ),
    )(displacement, force, damage, history, crack_flags)


def solution(mesh):
    return jax.shard_map(
        functools.partial(body, mesh.shape["gx"], mesh.shape["gy"]),
        mesh=mesh,
        in_specs=(
            P(None, "gx", "gy", None),
            P(None, "gx", "gy", None),
            P("gx", "gy", None),
            P("gx", "gy", None),
            P("gx", "gy", None),
        ),
        out_specs=(P(None, "gx", "gy", None), P("gx", "gy", None), P("gx", "gy", None)),
        check_vma=False,
    )
```

```python
import functools
import jax
import jax.numpy as jnp
from jax import lax
from jax.experimental import pallas as pl
from jax.experimental.pallas import tpu as pltpu
from jax.sharding import PartitionSpec as P

UNROLL = 4
SHIFT_U = 8.0
SHIFT_D = 15.0
XO = 2
XF = 3
RO = 8
DIRS = ((1, 0), (-1, 0), (0, 1), (0, -1), (1, 1), (1, -1), (-1, 1), (-1, -1))
MESH = pl.DeviceIdType.MESH
U_EX, D_EX, R_EX, W_EX, H_EX = range(5)
WIDTHS = {
    U_EX: (3, 1, 1, 1, 1),
    D_EX: (1, 2, 2, 2, 2),
    R_EX: (3, 2, 3, 2, 3),
    W_EX: (1, 2, 3, 2, 3),
    H_EX: (1, 1, 2, 1, 2),
}


def pieces(rows):
    return [(j, j, 1) for j in range(3)] if rows == 3 else [(0, 0, rows)]


def galerkin(total, shift):
    g00, g01, g02, g11, g12, g22, h22 = [total[k : k + 1, :] for k in range(7)]
    h00, h01, h02 = g01 + shift * g00, g11 + shift * g01, g12 + shift * g02
    h11, h12 = g12 + shift * g11, g22 + shift * g12
    l10, l20 = h01 / h00, h02 / h00
    d1 = h11 - l10 * h01
    e1 = h12 - l20 * h01
    l21 = e1 / d1
    f1 = h22 - l20 * h02 - l21 * e1
    z1 = g01 - l10 * g00
    z2 = g02 - l20 * g00 - l21 * z1
    y2 = jnp.where(f1 > 0.0, z2 / f1, 0.0)
    y1 = jnp.where(d1 > 0.0, z1 / d1 - l21 * y2, 0.0)
    y2 = jnp.where(d1 > 0.0, y2, 0.0)
    y0 = g00 / h00 - l10 * y1 - l20 * y2
    y0 = jnp.where(d1 > 0.0, y0, g00 / h00)
    return y0, y1, y2


def kernel(sizes, u_in, f_in, d_in, hist_in, crack_in, u_out, d_out, h_out, *scratch):
    n_gx, n_gy, X, Y, Z = sizes
    (U, V0, V1, V2, S, G, D, H, W0, W1, W2, F, HI, CR) = scratch[:14]
    stages = scratch[14:34]
    part, gath, send_sem, recv_sem, ar_send, ar_recv, loc_sem = scratch[34:]
    n = n_gx * n_gy
    gx, gy = lax.axis_index("gx"), lax.axis_index("gy")
    me = gx * n_gy + gy
    own_x, own_y = pl.ds(XO, X), pl.ds(RO, Y)

    loads = (
        pltpu.make_async_copy(u_in, U.at[:, own_x, own_y], loc_sem.at[0]),
        pltpu.make_async_copy(d_in, D.at[0, own_x, own_y], loc_sem.at[1]),
        pltpu.make_async_copy(f_in, F, loc_sem.at[2]),
        pltpu.make_async_copy(hist_in, HI, loc_sem.at[3]),
        pltpu.make_async_copy(crack_in, CR, loc_sem.at[4]),
    )
    for item in loads:
        item.start()

    def peer(i):
        t = lax.rem(me + i, n)
        return (t // n_gy, lax.rem(t, n_gy))

    barrier = pltpu.get_barrier_semaphore()

    def greet(i, c):
        pl.semaphore_signal(barrier, inc=1, device_id=peer(i), device_id_type=MESH)
        return c

    lax.fori_loop(1, n, greet, 0)

    def exists(dx, dy):
        ok = None
        for pos, size, d in ((gx, n_gx, dx), (gy, n_gy, dy)):
            if d:
                one = (pos + d < size) if d > 0 else (pos + d >= 0)
                ok = one if ok is None else jnp.logical_and(ok, one)
        return ok

    def copy_of(number, buf, k):
        comps, xb, xf, rb, rf = WIDTHS[number]
        send_b, send_f, got_b, got_f = stages[4 * number : 4 * number + 4]
        dx, dy = DIRS[k]
        sx = {1: pl.ds(XO + X - xb, xb), -1: pl.ds(XO, xf), 0: own_x}[dx]
        tx = {1: pl.ds(XO - xb, xb), -1: pl.ds(XO + X, xf), 0: own_x}[dx]
        if dy == 0:
            src, dst = buf.at[:, sx, own_y], buf.at[:, tx, own_y]
        elif dy > 0:
            src, dst = send_b.at[:, sx], got_b.at[:, tx]
        else:
            src, dst = send_f.at[:, sx], got_f.at[:, tx]
        return pltpu.make_async_remote_copy(
            src_ref=src,
            dst_ref=dst,
            send_sem=send_sem.at[number, k],
            recv_sem=recv_sem.at[number, k],
            device_id=(gx + dx, gy + dy),
            device_id_type=MESH,
        )

    def send(number, buf):
        comps, xb, xf, rb, rf = WIDTHS[number]
        send_b, send_f = stages[4 * number : 4 * number + 2]

        def go(k):
            pl.when(exists(*DIRS[k]))(lambda: copy_of(number, buf, k).start())

        def pack(x, c):
            for comp in range(comps):
                for j, at, w in pieces(rb):
                    r0 = RO + Y - rb + at
                    send_b[comp, x, j] = buf[comp, x, r0 : r0 + w, :]
                for j, at, w in pieces(rf):
                    r0 = RO + at
                    send_f[comp, x, j] = buf[comp, x, r0 : r0 + w, :]
            return c

        lax.fori_loop(XO, XO + X, pack, 0, unroll=UNROLL)
        for k in (4, 5, 6, 7, 2, 3, 0, 1):
            go(k)

    def receive(number, buf):
        comps, xb, xf, rb, rf = WIDTHS[number]
        got_b, got_f = stages[4 * number + 2 : 4 * number + 4]
        for k in range(8):
            dx, dy = DIRS[k]
            pl.when(exists(-dx, -dy))(lambda k=k: copy_of(number, buf, k).wait_recv())
        has_b, has_f = gy > 0, gy + 1 < n_gy

        def unpack(x, c):
            for comp in range(comps):
                for j, at, w in pieces(rb):
                    r0 = RO - rb + at
                    buf[comp, x, r0 : r0 + w, :] = jnp.where(has_b, got_b[comp, x, j], 0.0)
                for j, at, w in pieces(rf):
                    r0 = RO + Y + at
                    buf[comp, x, r0 : r0 + w, :] = jnp.where(has_f, got_f[comp, x, j], 0.0)
            return c

        lax.fori_loop(XO - xb, XO + X + xf, unpack, 0, unroll=UNROLL)
        rows = buf.shape[2]

        @pl.when(gx == 0)
        def _():
            buf[:, XO - xb : XO] = jnp.zeros((comps, xb, rows, Z), jnp.float32)

        @pl.when(gx == n_gx - 1)
        def _():
            buf[:, XO + X : XO + X + xf] = jnp.zeros((comps, xf, rows, Z), jnp.float32)

    def sent(number, buf):
        for k in range(8):
            pl.when(exists(*DIRS[k]))(lambda k=k: copy_of(number, buf, k).wait_send())

    def lanes(rows):
        return lax.broadcasted_iota(jnp.int32, (rows, Z), 1)

    def next_z(a):
        return jnp.where(lanes(a.shape[0]) == Z - 1, 0.0, pltpu.roll(a, Z - 1, 1))

    def last_z(a):
        return jnp.where(lanes(a.shape[0]) == 0, 0.0, pltpu.roll(a, 1, 1))

    def inside(x, r0, rows):
        at = lax.broadcasted_iota(jnp.int32, (rows, Z), 0) + (gy * Y + (r0 - RO))
        xg = gx * X + (x - XO)
        top = jnp.where(jnp.logical_and(xg >= 0, xg < n_gx * X), n_gy * Y, 0)
        return jnp.logical_and(at >= 0, at < top)

    def grads(src, x, r0, rows):
        here = [src[c, x, r0 : r0 + rows, :] for c in range(3)]
        result = []
        for c in range(3):
            result.append(
                (
                    src[c, x + 1, r0 : r0 + rows, :] - here[c],
                    src[c, x, r0 + 1 : r0 + 1 + rows, :] - here[c],
                    next_z(here[c]) - here[c],
                )
            )
        return here, result

    def stress(src, x, r0, rows):
        here, d = grads(src, x, r0, rows)
        g = G[x, r0 : r0 + rows, :]
        g2 = g + g
        lam = (1.5 * g) * (d[0][0] + d[1][1] + d[2][2])
        S[0, x, r0 : r0 + rows, :] = g2 * d[0][0] + lam
        S[1, x, r0 : r0 + rows, :] = g2 * d[1][1] + lam
        S[2, x, r0 : r0 + rows, :] = g2 * d[2][2] + lam
        S[3, x, r0 : r0 + rows, :] = g * (d[0][1] + d[1][0])
        S[4, x, r0 : r0 + rows, :] = g * (d[0][2] + d[2][0])
        S[5, x, r0 : r0 + rows, :] = g * (d[1][2] + d[2][1])

    index = ((0, 3, 4), (3, 1, 5), (4, 5, 2))

    def divergence(src, x, r0, rows, spring):
        at = [S[k, x, r0 : r0 + rows, :] for k in range(6)]
        images = []
        for c in range(3):
            ix, iy, iz = index[c]
            total = spring * src[c, x, r0 : r0 + rows, :]
            total = total + (S[ix, x - 1, r0 : r0 + rows, :] - at[ix])
            total = total + (S[iy, x, r0 - 1 : r0 - 1 + rows, :] - at[iy])
            total = total + (last_z(at[iz]) - at[iz])
            images.append(total)
        return images

    def apply_elastic(src, dst, x0, x1, r0, rows, s_rows):
        spring = 0.5 if dst is V0 else 0.5 - SHIFT_U

        def strain_step(x, c):
            stress(src, x, r0 - 1, s_rows)
            return c

        lax.fori_loop(x0 - 1, x1, strain_step, 0, unroll=UNROLL)

        def step(x, c):
            images = divergence(src, x, r0, rows, spring)
            if dst is V0:
                for comp in range(3):
                    V0[comp, x, r0 : r0 + rows, :] = F[comp, x - XO] - images[comp]
            else:
                ok = inside(x, r0, rows)
                for comp in range(3):
                    dst[comp, x, r0 : r0 + rows, :] = jnp.where(ok, images[comp], 0.0)
            return c

        lax.fori_loop(x0, x1, step, 0, unroll=UNROLL)

    def fold(a):
        total = a[0:8]
        for k in range(1, a.shape[0] // 8):
            total = total + a[8 * k : 8 * k + 8]
        return total

    def all_sum(number, accs):
        lane = lax.broadcasted_iota(jnp.int32, (1, Z), 1)
        row = jnp.zeros((1, Z), jnp.float32)
        for k, a in enumerate(accs):
            one = jnp.sum(jnp.sum(a, axis=0, keepdims=True), axis=1, keepdims=True)
            row = jnp.where(lane == k, one, row)
        part[number, 0] = row
        gath[number, me] = row

        def go(i, c):
            pltpu.make_async_remote_copy(
                src_ref=part.at[number, 0],
                dst_ref=gath.at[number, me],
                send_sem=ar_send.at[number],
                recv_sem=ar_recv.at[number],
                device_id=peer(i),
                device_id_type=MESH,
            ).start()
            return c

        lax.fori_loop(1, n, go, 0)

    def all_wait(number, shift):
        whole = gath.at[number, pl.ds(0, n - 1)]
        pltpu.make_async_copy(whole, whole, ar_recv.at[number]).wait()
        pltpu.make_async_copy(whole, whole, ar_send.at[number]).wait()
        row = jnp.sum(gath[number], axis=0)
        wide = jnp.broadcast_to(row, (8, Z))
        diag = lax.broadcasted_iota(jnp.int32, (8, Z), 0) == lanes(8)
        column = jnp.sum(jnp.where(diag, wide, 0.0), axis=1, keepdims=True)
        return galerkin(jnp.broadcast_to(column, (8, Z)), shift)

    loads[0].wait()
    loads[1].wait()
    pl.semaphore_wait(barrier, n - 1)
    send(U_EX, U)
    send(D_EX, D)
    receive(D_EX, D)
    all_rows = RO + Y + RO

    def make_gain(x, c):
        left = 1.0 - D[0, x]
        G[x] = jnp.where(inside(x, 0, all_rows), left * left + 0.001, 0.0)
        return c

    lax.fori_loop(XO - 2, XO + X + 2, make_gain, 0, unroll=UNROLL)
    loads[2].wait()
    receive(U_EX, U)
    apply_elastic(U, V0, XO, XO + X, RO, Y, Y + 8)
    send(R_EX, V0)
    loads[3].wait()
    loads[4].wait()
    receive(R_EX, V0)
    apply_elastic(V0, V1, XO - 1, XO + X + 2, RO - 1, Y + 8, Y + 8)
    apply_elastic(V1, V2, XO, XO + X + 1, RO - 1, Y + 8, Y + 8)

    def moments(x, accs):
        here, d = grads(V2, x, RO, Y)
        g = G[x, RO : RO + Y, :]
        tr = d[0][0] + d[1][1] + d[2][2]
        s01, s02, s12 = d[0][1] + d[1][0], d[0][2] + d[2][0], d[1][2] + d[2][1]
        normal = d[0][0] * d[0][0] + d[1][1] * d[1][1] + d[2][2] * d[2][2]
        energy = g * (2.0 * normal + (s01 * s01 + s02 * s02 + s12 * s12) + 1.5 * tr * tr)
        v0 = [V0[c, x, RO : RO + Y, :] for c in range(3)]
        v1 = [V1[c, x, RO : RO + Y, :] for c in range(3)]

        def dot(a, b):
            return a[0] * b[0] + a[1] * b[1] + a[2] * b[2]

        m4 = dot(here, here)
        terms = (dot(v0, v0), dot(v0, v1), dot(v0, here), dot(v1, v1))
        terms = terms + (dot(v1, here), m4, energy + 0.5 * m4)
        return tuple(acc + fold(term) for acc, term in zip(accs, terms))

    zero = tuple(jnp.zeros((8, Z), jnp.float32) for _ in range(7))
    all_sum(0, lax.fori_loop(XO, XO + X, moments, zero, unroll=2))
    sent(U_EX, U)
    sent(R_EX, V0)
    sent(D_EX, D)
    y0, y1, y2 = all_wait(0, SHIFT_U)

    def move(x, c):
        for comp in range(3):
            rows = pl.ds(RO, Y + 8)
            U[comp, x, rows, :] = (
                U[comp, x, rows, :]
                + y0 * V0[comp, x, rows, :]
                + y1 * V1[comp, x, rows, :]
                + y2 * V2[comp, x, rows, :]
            )
        return c

    lax.fori_loop(XO, XO + X + 1, move, 0, unroll=2)
    u_store = pltpu.make_async_copy(U.at[:, own_x, own_y], u_out, loc_sem.at[5])
    u_store.start()

    def beside(src, x, r0, rows):
        here = src[0, x, r0 : r0 + rows, :]
        ahead = src[0, x + 1, r0 : r0 + rows, :] + src[0, x, r0 + 1 : r0 + 1 + rows, :] + next_z(here)
        behind = src[0, x - 1, r0 : r0 + rows, :] + src[0, x, r0 - 1 : r0 - 1 + rows, :] + last_z(here)
        return here, ahead, behind

    def drive(x, c):
        here, d = grads(U, x, RO, Y)
        tr = d[0][0] + d[1][1] + d[2][2]
        s01, s02, s12 = d[0][1] + d[1][0], d[0][2] + d[2][0], d[1][2] + d[2][1]
        squares = d[0][0] * d[0][0] + d[1][1] * d[1][1] + d[2][2] * d[2][2]
        squares = squares + 0.5 * (s01 * s01 + s02 * s02 + s12 * s12)
        up = jnp.maximum(tr, 0.0)
        psi = (0.5 * (1.5 + 2.0 / 3.0)) * up * up + (squares - tr * tr * (1.0 / 3.0))
        flags = 4.0 * CR[x - XO].astype(jnp.float32)
        h = jnp.maximum(jnp.maximum(HI[x - XO], psi), flags)
        H[0, x, RO : RO + Y, :] = h
        now, ahead, behind = beside(D, x, RO, Y)
        image = (0.5 + 2.0 * h) * now + 2.0 * (6.0 * now - (ahead + behind))
        W0[0, x, RO : RO + Y, :] = 2.0 * h - image
        return c

    lax.fori_loop(XO, XO + X, drive, 0, unroll=2)
    send(W_EX, W0)
    send(H_EX, H)
    h_store = pltpu.make_async_copy(H.at[0, own_x, own_y], h_out, loc_sem.at[6])
    h_store.start()
    receive(W_EX, W0)
    receive(H_EX, H)

    def apply_damage(src, dst, x0, x1):
        r0, rows = RO - 1, Y + 8

        def step(x, c):
            here, ahead, behind = beside(src, x, r0, rows)
            h = H[0, x, r0 : r0 + rows, :]
            image = ((12.5 - SHIFT_D) + 2.0 * h) * here - 2.0 * (ahead + behind)
            dst[0, x, r0 : r0 + rows, :] = jnp.where(inside(x, r0, rows), image, 0.0)
            return c

        lax.fori_loop(x0, x1, step, 0, unroll=UNROLL)

    apply_damage(W0, W1, XO - 1, XO + X + 2)
    apply_damage(W1, W2, XO, XO + X + 1)

    def damage_moments(x, accs):
        w2 = W2[0, x, RO : RO + Y, :]
        ahead = W2[0, x + 1, RO : RO + Y, :] + W2[0, x, RO + 1 : RO + 1 + Y, :] + next_z(w2)
        w0, w1 = W0[0, x, RO : RO + Y, :], W1[0, x, RO : RO + Y, :]
        m5 = w2 * ((12.5 + 2.0 * H[0, x, RO : RO + Y, :]) * w2 - 4.0 * ahead)
        terms = (w0 * w0, w0 * w1, w0 * w2, w1 * w1, w1 * w2, w2 * w2, m5)
        return tuple(acc + fold(term) for acc, term in zip(accs, terms))

    all_sum(1, lax.fori_loop(XO, XO + X, damage_moments, zero, unroll=2))
    sent(W_EX, W0)
    sent(H_EX, H)
    y0, y1, y2 = all_wait(1, SHIFT_D)

    def heal(x, c):
        rows = pl.ds(RO, Y)
        D[0, x, rows, :] = (
            D[0, x, rows, :]
            + y0 * W0[0, x, rows, :]
            + y1 * W1[0, x, rows, :]
            + y2 * W2[0, x, rows, :]
        )
        return c

    lax.fori_loop(XO, XO + X, heal, 0, unroll=UNROLL)
    d_store = pltpu.make_async_copy(D.at[0, own_x, own_y], d_out, loc_sem.at[7])
    d_store.start()
    u_store.wait()
    h_store.wait()
    d_store.wait()


def store_results(u, d, h, u_out, d_out, h_out, sem):
    pairs = ((u, u_out), (d, d_out), (h, h_out))
    copies = [pltpu.make_async_copy(a, b, sem.at[k]) for k, (a, b) in enumerate(pairs)]
    for item in copies:
        item.start()
    for item in copies:
        item.wait()


def body(n_gx, n_gy, displacement, force, damage, history, crack_flags):
    _, X, Y, Z = displacement.shape
    slabs, rows = XO + X + XF, RO + Y + RO
    n = n_gx * n_gy
    f32 = jnp.float32

    def field(comps):
        return pltpu.VMEM((comps, slabs, rows, Z), f32)

    scratch = [field(3)] * 4 + [field(6), pltpu.VMEM((slabs, rows, Z), f32)]
    scratch += [field(1)] * 5
    scratch += [
        pltpu.VMEM((3, X, Y, Z), f32),
        pltpu.VMEM((X, Y, Z), f32),
        pltpu.VMEM((X, Y, Z), crack_flags.dtype),
    ]
    for number in range(5):
        comps, xb, xf, rb, rf = WIDTHS[number]
        for r in (rb, rf, rb, rf):
            parts = pieces(r)
            scratch.append(pltpu.VMEM((comps, slabs, len(parts), parts[0][2], Z), f32))
    scratch += [
        pltpu.VMEM((2, 1, 1, Z), f32),
        pltpu.VMEM((2, n, 1, Z), f32),
        pltpu.SemaphoreType.DMA((5, 8)),
        pltpu.SemaphoreType.DMA((5, 8)),
        pltpu.SemaphoreType.DMA((2,)),
        pltpu.SemaphoreType.DMA((2,)),
        pltpu.SemaphoreType.DMA((8,)),
    ]
    scalar = jax.ShapeDtypeStruct((X, Y, Z), f32)
    given = (displacement, force, damage, history, crack_flags)
    results = pl.pallas_call(
        functools.partial(kernel, (n_gx, n_gy, X, Y, Z)),
        out_shape=tuple(pltpu.VMEM(a.shape, f32) for a in (displacement, damage, history)),
        in_specs=[pl.BlockSpec(memory_space=pltpu.HBM)] * 5,
        out_specs=tuple([pl.BlockSpec(memory_space=pl.ANY)] * 3),
        scratch_shapes=scratch,
        compiler_params=pltpu.CompilerParams(
            collective_id=0, has_side_effects=True, vmem_limit_bytes=48 * 1024 * 1024
        ),
    )(*[pltpu.with_memory_space_constraint(a, pltpu.HBM) for a in given])
    return pl.pallas_call(
        store_results,
        out_shape=(jax.ShapeDtypeStruct(displacement.shape, f32), scalar, scalar),
        in_specs=[pl.BlockSpec(memory_space=pltpu.VMEM)] * 3,
        out_specs=tuple([pl.BlockSpec(memory_space=pl.ANY)] * 3),
        scratch_shapes=[pltpu.SemaphoreType.DMA((3,))],
    )(*[pltpu.with_memory_space_constraint(a, pltpu.VMEM) for a in results])


def solution(mesh):
    return jax.shard_map(
        functools.partial(body, mesh.shape["gx"], mesh.shape["gy"]),
        mesh=mesh,
        in_specs=(
            P(None, "gx", "gy", None),
            P(None, "gx", "gy", None),
            P("gx", "gy", None),
            P("gx", "gy", None),
            P("gx", "gy", None),
        ),
        out_specs=(P(None, "gx", "gy", None), P("gx", "gy", None), P("gx", "gy", None)),
        check_vma=False,
    )
```

```python
import functools
import jax
import jax.numpy as jnp
from jax import lax
from jax.experimental import pallas as pl
from jax.experimental.pallas import tpu as pltpu
from jax.sharding import PartitionSpec as P

UNROLL = 8
SHIFT_U = 8.0
SHIFT_D = 15.0
XO = 2
XF = 3
RO = 8
DIRS = ((1, 0), (-1, 0), (0, 1), (0, -1), (1, 1), (1, -1), (-1, 1), (-1, -1))
MESH = pl.DeviceIdType.MESH
U_EX, D_EX, R_EX, W_EX, H_EX = range(5)
WIDTHS = {
    U_EX: (3, 1, 1, 1, 1),
    D_EX: (1, 2, 2, 2, 2),
    R_EX: (3, 2, 3, 2, 3),
    W_EX: (1, 2, 3, 2, 3),
    H_EX: (1, 1, 2, 1, 2),
}


def pieces(rows):
    return [(j, j, 1) for j in range(3)] if rows == 3 else [(0, 0, rows)]


def galerkin(total, shift):
    g00, g01, g02, g11, g12, g22, h22 = [total[k : k + 1, :] for k in range(7)]
    h00, h01, h02 = g01 + shift * g00, g11 + shift * g01, g12 + shift * g02
    h11, h12 = g12 + shift * g11, g22 + shift * g12
    l10, l20 = h01 / h00, h02 / h00
    d1 = h11 - l10 * h01
    e1 = h12 - l20 * h01
    l21 = e1 / d1
    f1 = h22 - l20 * h02 - l21 * e1
    z1 = g01 - l10 * g00
    z2 = g02 - l20 * g00 - l21 * z1
    y2 = jnp.where(f1 > 0.0, z2 / f1, 0.0)
    y1 = jnp.where(d1 > 0.0, z1 / d1 - l21 * y2, 0.0)
    y2 = jnp.where(d1 > 0.0, y2, 0.0)
    y0 = g00 / h00 - l10 * y1 - l20 * y2
    y0 = jnp.where(d1 > 0.0, y0, g00 / h00)
    return y0, y1, y2


def kernel(sizes, u_in, f_in, d_in, hist_in, crack_in, u_out, d_out, h_out, *scratch):
    n_gx, n_gy, X, Y, Z = sizes
    (U, V0, V1, V2, S, G, D, H, W0, W1, W2, F, HI, CR) = scratch[:14]
    stages = scratch[14:34]
    part, gath, send_sem, recv_sem, ar_send, ar_recv, loc_sem = scratch[34:]
    n = n_gx * n_gy
    gx, gy = lax.axis_index("gx"), lax.axis_index("gy")
    me = gx * n_gy + gy
    own_x, own_y = pl.ds(XO, X), pl.ds(RO, Y)

    loads = (
        pltpu.make_async_copy(u_in, U.at[:, own_x, own_y], loc_sem.at[0]),
        pltpu.make_async_copy(d_in, D.at[0, own_x, own_y], loc_sem.at[1]),
        pltpu.make_async_copy(f_in, F, loc_sem.at[2]),
        pltpu.make_async_copy(hist_in, HI, loc_sem.at[3]),
        pltpu.make_async_copy(crack_in, CR, loc_sem.at[4]),
    )
    for item in loads:
        item.start()

    def each_peer(act):
        def wrapped(at, size):
            return jnp.where(at >= size, at - size, at)

        ys = [wrapped(gy + dy, n_gy) for dy in range(n_gy)]

        def column(dx, c):
            tx = wrapped(gx + dx, n_gx)
            for ty in ys:
                act((tx, ty))
            return c

        for ty in ys[1:]:
            act((gx, ty))
        lax.fori_loop(1, n_gx, column, 0)

    barrier = pltpu.get_barrier_semaphore()

    def greet(device):
        pl.semaphore_signal(barrier, inc=1, device_id=device, device_id_type=MESH)

    each_peer(greet)

    def exists(dx, dy):
        ok = None
        for pos, size, d in ((gx, n_gx, dx), (gy, n_gy, dy)):
            if d:
                one = (pos + d < size) if d > 0 else (pos + d >= 0)
                ok = one if ok is None else jnp.logical_and(ok, one)
        return ok

    def copy_of(number, buf, k):
        comps, xb, xf, rb, rf = WIDTHS[number]
        send_b, send_f, got_b, got_f = stages[4 * number : 4 * number + 4]
        dx, dy = DIRS[k]
        sx = {1: pl.ds(XO + X - xb, xb), -1: pl.ds(XO, xf), 0: own_x}[dx]
        tx = {1: pl.ds(XO - xb, xb), -1: pl.ds(XO + X, xf), 0: own_x}[dx]
        if dy == 0:
            src, dst = buf.at[:, sx, own_y], buf.at[:, tx, own_y]
        elif dy > 0:
            src, dst = send_b.at[:, sx], got_b.at[:, tx]
        else:
            src, dst = send_f.at[:, sx], got_f.at[:, tx]
        return pltpu.make_async_remote_copy(
            src_ref=src,
            dst_ref=dst,
            send_sem=send_sem.at[number, k],
            recv_sem=recv_sem.at[number, k],
            device_id=(gx + dx, gy + dy),
            device_id_type=MESH,
        )

    def send(number, buf):
        comps, xb, xf, rb, rf = WIDTHS[number]
        send_b, send_f = stages[4 * number : 4 * number + 2]

        def go(k):
            pl.when(exists(*DIRS[k]))(lambda: copy_of(number, buf, k).start())

        def pack(x, c):
            for comp in range(comps):
                for j, at, w in pieces(rb):
                    r0 = RO + Y - rb + at
                    send_b[comp, x, j] = buf[comp, x, r0 : r0 + w, :]
                for j, at, w in pieces(rf):
                    r0 = RO + at
                    send_f[comp, x, j] = buf[comp, x, r0 : r0 + w, :]
            return c

        go(0)
        go(1)
        lax.fori_loop(XO, XO + X, pack, 0, unroll=UNROLL)
        for k in (4, 5, 6, 7, 2, 3):
            go(k)

    def receive(number, buf):
        comps, xb, xf, rb, rf = WIDTHS[number]
        got_b, got_f = stages[4 * number + 2 : 4 * number + 4]
        for k in range(8):
            dx, dy = DIRS[k]
            pl.when(exists(-dx, -dy))(lambda k=k: copy_of(number, buf, k).wait_recv())
        has_b, has_f = gy > 0, gy + 1 < n_gy

        def unpack(x, c):
            for comp in range(comps):
                for j, at, w in pieces(rb):
                    r0 = RO - rb + at
                    buf[comp, x, r0 : r0 + w, :] = jnp.where(has_b, got_b[comp, x, j], 0.0)
                for j, at, w in pieces(rf):
                    r0 = RO + Y + at
                    buf[comp, x, r0 : r0 + w, :] = jnp.where(has_f, got_f[comp, x, j], 0.0)
            return c

        lax.fori_loop(XO - xb, XO + X + xf, unpack, 0, unroll=UNROLL)
        rows = buf.shape[2]

        @pl.when(gx == 0)
        def _():
            buf[:, XO - xb : XO] = jnp.zeros((comps, xb, rows, Z), jnp.float32)

        @pl.when(gx == n_gx - 1)
        def _():
            buf[:, XO + X : XO + X + xf] = jnp.zeros((comps, xf, rows, Z), jnp.float32)

    def sent(number, buf):
        for k in range(8):
            pl.when(exists(*DIRS[k]))(lambda k=k: copy_of(number, buf, k).wait_send())

    def lanes(rows):
        return lax.broadcasted_iota(jnp.int32, (rows, Z), 1)

    def next_z(a):
        return jnp.where(lanes(a.shape[0]) == Z - 1, 0.0, pltpu.roll(a, Z - 1, 1))

    def last_z(a):
        return jnp.where(lanes(a.shape[0]) == 0, 0.0, pltpu.roll(a, 1, 1))

    def inside(x, r0, rows):
        at = lax.broadcasted_iota(jnp.int32, (rows, Z), 0) + (gy * Y + (r0 - RO))
        xg = gx * X + (x - XO)
        top = jnp.where(jnp.logical_and(xg >= 0, xg < n_gx * X), n_gy * Y, 0)
        return jnp.logical_and(at >= 0, at < top)

    def grads(src, x, r0, rows):
        here = [src[c, x, r0 : r0 + rows, :] for c in range(3)]
        result = []
        for c in range(3):
            result.append(
                (
                    src[c, x + 1, r0 : r0 + rows, :] - here[c],
                    src[c, x, r0 + 1 : r0 + 1 + rows, :] - here[c],
                    next_z(here[c]) - here[c],
                )
            )
        return here, result

    def stress(src, x, r0, rows):
        here, d = grads(src, x, r0, rows)
        g = G[x, r0 : r0 + rows, :]
        g2 = g + g
        lam = (1.5 * g) * (d[0][0] + d[1][1] + d[2][2])
        S[0, x, r0 : r0 + rows, :] = g2 * d[0][0] + lam
        S[1, x, r0 : r0 + rows, :] = g2 * d[1][1] + lam
        S[2, x, r0 : r0 + rows, :] = g2 * d[2][2] + lam
        S[3, x, r0 : r0 + rows, :] = g * (d[0][1] + d[1][0])
        S[4, x, r0 : r0 + rows, :] = g * (d[0][2] + d[2][0])
        S[5, x, r0 : r0 + rows, :] = g * (d[1][2] + d[2][1])

    index = ((0, 3, 4), (3, 1, 5), (4, 5, 2))

    def divergence(src, x, r0, rows, spring):
        at = [S[k, x, r0 : r0 + rows, :] for k in range(6)]
        images = []
        for c in range(3):
            ix, iy, iz = index[c]
            total = spring * src[c, x, r0 : r0 + rows, :]
            total = total + (S[ix, x - 1, r0 : r0 + rows, :] - at[ix])
            total = total + (S[iy, x, r0 - 1 : r0 - 1 + rows, :] - at[iy])
            total = total + (last_z(at[iz]) - at[iz])
            images.append(total)
        return images

    def apply_elastic(src, dst, x0, x1, r0, rows, s_rows):
        spring = 0.5 if dst is V0 else 0.5 - SHIFT_U

        def strain_step(x, c):
            stress(src, x, r0 - 1, s_rows)
            return c

        lax.fori_loop(x0 - 1, x1, strain_step, 0, unroll=UNROLL)

        def step(x, c):
            images = divergence(src, x, r0, rows, spring)
            if dst is V0:
                for comp in range(3):
                    V0[comp, x, r0 : r0 + rows, :] = F[comp, x - XO] - images[comp]
            else:
                ok = inside(x, r0, rows)
                for comp in range(3):
                    dst[comp, x, r0 : r0 + rows, :] = jnp.where(ok, images[comp], 0.0)
            return c

        lax.fori_loop(x0, x1, step, 0, unroll=UNROLL)

    def fold(a):
        total = a[0:8]
        for k in range(1, a.shape[0] // 8):
            total = total + a[8 * k : 8 * k + 8]
        return total

    def all_sum(number, accs):
        lane = lax.broadcasted_iota(jnp.int32, (1, Z), 1)
        row = jnp.zeros((1, Z), jnp.float32)
        for k, a in enumerate(accs):
            one = jnp.sum(jnp.sum(a, axis=0, keepdims=True), axis=1, keepdims=True)
            row = jnp.where(lane == k, one, row)
        part[number, 0] = row
        gath[number, me] = row

        def go(device):
            pltpu.make_async_remote_copy(
                src_ref=part.at[number, 0],
                dst_ref=gath.at[number, me],
                send_sem=ar_send.at[number],
                recv_sem=ar_recv.at[number],
                device_id=device,
                device_id_type=MESH,
            ).start()

        each_peer(go)

    def all_wait(number, shift):
        whole = gath.at[number, pl.ds(0, n - 1)]
        pltpu.make_async_copy(whole, whole, ar_recv.at[number]).wait()
        pltpu.make_async_copy(whole, whole, ar_send.at[number]).wait()
        row = jnp.sum(gath[number], axis=0)
        wide = jnp.broadcast_to(row, (8, Z))
        diag = lax.broadcasted_iota(jnp.int32, (8, Z), 0) == lanes(8)
        column = jnp.sum(jnp.where(diag, wide, 0.0), axis=1, keepdims=True)
        return galerkin(jnp.broadcast_to(column, (8, Z)), shift)

    loads[0].wait()
    loads[1].wait()
    pl.semaphore_wait(barrier, n - 1)
    send(U_EX, U)
    send(D_EX, D)
    receive(D_EX, D)
    all_rows = RO + Y + RO

    def make_gain(x, c):
        left = 1.0 - D[0, x]
        G[x] = jnp.where(inside(x, 0, all_rows), left * left + 0.001, 0.0)
        return c

    lax.fori_loop(XO - 2, XO + X + 2, make_gain, 0, unroll=UNROLL)
    loads[2].wait()
    receive(U_EX, U)
    apply_elastic(U, V0, XO, XO + X, RO, Y, Y + 8)
    send(R_EX, V0)
    loads[3].wait()
    loads[4].wait()
    receive(R_EX, V0)
    apply_elastic(V0, V1, XO - 1, XO + X + 2, RO - 1, Y + 8, Y + 8)
    apply_elastic(V1, V2, XO, XO + X + 1, RO - 1, Y + 8, Y + 8)

    def moments(x, accs):
        here, d = grads(V2, x, RO, Y)
        g = G[x, RO : RO + Y, :]
        tr = d[0][0] + d[1][1] + d[2][2]
        s01, s02, s12 = d[0][1] + d[1][0], d[0][2] + d[2][0], d[1][2] + d[2][1]
        normal = d[0][0] * d[0][0] + d[1][1] * d[1][1] + d[2][2] * d[2][2]
        energy = g * (2.0 * normal + (s01 * s01 + s02 * s02 + s12 * s12) + 1.5 * tr * tr)
        v0 = [V0[c, x, RO : RO + Y, :] for c in range(3)]
        v1 = [V1[c, x, RO : RO + Y, :] for c in range(3)]

        def dot(a, b):
            return a[0] * b[0] + a[1] * b[1] + a[2] * b[2]

        m4 = dot(here, here)
        terms = (dot(v0, v0), dot(v0, v1), dot(v0, here), dot(v1, v1))
        terms = terms + (dot(v1, here), m4, energy + 0.5 * m4)
        return tuple(acc + fold(term) for acc, term in zip(accs, terms))

    zero = tuple(jnp.zeros((8, Z), jnp.float32) for _ in range(7))
    all_sum(0, lax.fori_loop(XO, XO + X, moments, zero, unroll=4))
    sent(U_EX, U)
    sent(R_EX, V0)
    sent(D_EX, D)
    y0, y1, y2 = all_wait(0, SHIFT_U)

    def move(x, c):
        for comp in range(3):
            rows = pl.ds(RO, Y + 8)
            U[comp, x, rows, :] = (
                U[comp, x, rows, :]
                + y0 * V0[comp, x, rows, :]
                + y1 * V1[comp, x, rows, :]
                + y2 * V2[comp, x, rows, :]
            )
        return c

    lax.fori_loop(XO, XO + X + 1, move, 0, unroll=4)
    u_store = pltpu.make_async_copy(U.at[:, own_x, own_y], u_out, loc_sem.at[5])
    u_store.start()

    def beside(src, x, r0, rows):
        here = src[0, x, r0 : r0 + rows, :]
        ahead = src[0, x + 1, r0 : r0 + rows, :] + src[0, x, r0 + 1 : r0 + 1 + rows, :] + next_z(here)
        behind = src[0, x - 1, r0 : r0 + rows, :] + src[0, x, r0 - 1 : r0 - 1 + rows, :] + last_z(here)
        return here, ahead, behind

    def drive(x, c):
        here, d = grads(U, x, RO, Y)
        tr = d[0][0] + d[1][1] + d[2][2]
        s01, s02, s12 = d[0][1] + d[1][0], d[0][2] + d[2][0], d[1][2] + d[2][1]
        squares = d[0][0] * d[0][0] + d[1][1] * d[1][1] + d[2][2] * d[2][2]
        squares = squares + 0.5 * (s01 * s01 + s02 * s02 + s12 * s12)
        up = jnp.maximum(tr, 0.0)
        psi = (0.5 * (1.5 + 2.0 / 3.0)) * up * up + (squares - tr * tr * (1.0 / 3.0))
        flags = 4.0 * CR[x - XO].astype(jnp.float32)
        h = jnp.maximum(jnp.maximum(HI[x - XO], psi), flags)
        H[0, x, RO : RO + Y, :] = h
        now, ahead, behind = beside(D, x, RO, Y)
        image = (0.5 + 2.0 * h) * now + 2.0 * (6.0 * now - (ahead + behind))
        W0[0, x, RO : RO + Y, :] = 2.0 * h - image
        return c

    lax.fori_loop(XO, XO + X, drive, 0, unroll=4)
    send(W_EX, W0)
    send(H_EX, H)
    h_store = pltpu.make_async_copy(H.at[0, own_x, own_y], h_out, loc_sem.at[6])
    h_store.start()
    receive(W_EX, W0)
    receive(H_EX, H)

    def apply_damage(src, dst, x0, x1):
        r0, rows = RO - 1, Y + 8

        def step(x, c):
            here, ahead, behind = beside(src, x, r0, rows)
            h = H[0, x, r0 : r0 + rows, :]
            image = ((12.5 - SHIFT_D) + 2.0 * h) * here - 2.0 * (ahead + behind)
            dst[0, x, r0 : r0 + rows, :] = jnp.where(inside(x, r0, rows), image, 0.0)
            return c

        lax.fori_loop(x0, x1, step, 0, unroll=UNROLL)

    apply_damage(W0, W1, XO - 1, XO + X + 2)
    apply_damage(W1, W2, XO, XO + X + 1)

    def damage_moments(x, accs):
        w2 = W2[0, x, RO : RO + Y, :]
        ahead = W2[0, x + 1, RO : RO + Y, :] + W2[0, x, RO + 1 : RO + 1 + Y, :] + next_z(w2)
        w0, w1 = W0[0, x, RO : RO + Y, :], W1[0, x, RO : RO + Y, :]
        m5 = w2 * ((12.5 + 2.0 * H[0, x, RO : RO + Y, :]) * w2 - 4.0 * ahead)
        terms = (w0 * w0, w0 * w1, w0 * w2, w1 * w1, w1 * w2, w2 * w2, m5)
        return tuple(acc + fold(term) for acc, term in zip(accs, terms))

    all_sum(1, lax.fori_loop(XO, XO + X, damage_moments, zero, unroll=4))
    sent(W_EX, W0)
    sent(H_EX, H)
    y0, y1, y2 = all_wait(1, SHIFT_D)

    def heal(x, c):
        rows = pl.ds(RO, Y)
        D[0, x, rows, :] = (
            D[0, x, rows, :]
            + y0 * W0[0, x, rows, :]
            + y1 * W1[0, x, rows, :]
            + y2 * W2[0, x, rows, :]
        )
        return c

    lax.fori_loop(XO, XO + X, heal, 0, unroll=UNROLL)
    d_store = pltpu.make_async_copy(D.at[0, own_x, own_y], d_out, loc_sem.at[7])
    d_store.start()
    u_store.wait()
    h_store.wait()
    d_store.wait()


def store_results(u, d, h, u_out, d_out, h_out, sem):
    pairs = ((u, u_out), (d, d_out), (h, h_out))
    copies = [pltpu.make_async_copy(a, b, sem.at[k]) for k, (a, b) in enumerate(pairs)]
    for item in copies:
        item.start()
    for item in copies:
        item.wait()


def body(n_gx, n_gy, displacement, force, damage, history, crack_flags):
    _, X, Y, Z = displacement.shape
    slabs, rows = XO + X + XF, RO + Y + RO
    n = n_gx * n_gy
    f32 = jnp.float32

    def field(comps):
        return pltpu.VMEM((comps, slabs, rows, Z), f32)

    scratch = [field(3)] * 4 + [field(6), pltpu.VMEM((slabs, rows, Z), f32)]
    scratch += [field(1)] * 5
    scratch += [
        pltpu.VMEM((3, X, Y, Z), f32),
        pltpu.VMEM((X, Y, Z), f32),
        pltpu.VMEM((X, Y, Z), crack_flags.dtype),
    ]
    for number in range(5):
        comps, xb, xf, rb, rf = WIDTHS[number]
        for r in (rb, rf, rb, rf):
            parts = pieces(r)
            scratch.append(pltpu.VMEM((comps, slabs, len(parts), parts[0][2], Z), f32))
    scratch += [
        pltpu.VMEM((2, 1, 1, Z), f32),
        pltpu.VMEM((2, n, 1, Z), f32),
        pltpu.SemaphoreType.DMA((5, 8)),
        pltpu.SemaphoreType.DMA((5, 8)),
        pltpu.SemaphoreType.DMA((2,)),
        pltpu.SemaphoreType.DMA((2,)),
        pltpu.SemaphoreType.DMA((8,)),
    ]
    scalar = jax.ShapeDtypeStruct((X, Y, Z), f32)
    given = (displacement, force, damage, history, crack_flags)
    results = pl.pallas_call(
        functools.partial(kernel, (n_gx, n_gy, X, Y, Z)),
        out_shape=tuple(pltpu.VMEM(a.shape, f32) for a in (displacement, damage, history)),
        in_specs=[pl.BlockSpec(memory_space=pltpu.HBM)] * 5,
        out_specs=tuple([pl.BlockSpec(memory_space=pl.ANY)] * 3),
        scratch_shapes=scratch,
        compiler_params=pltpu.CompilerParams(
            collective_id=0, has_side_effects=True, vmem_limit_bytes=48 * 1024 * 1024
        ),
    )(*[pltpu.with_memory_space_constraint(a, pltpu.HBM) for a in given])
    return pl.pallas_call(
        store_results,
        out_shape=(jax.ShapeDtypeStruct(displacement.shape, f32), scalar, scalar),
        in_specs=[pl.BlockSpec(memory_space=pltpu.VMEM)] * 3,
        out_specs=tuple([pl.BlockSpec(memory_space=pl.ANY)] * 3),
        scratch_shapes=[pltpu.SemaphoreType.DMA((3,))],
    )(*[pltpu.with_memory_space_constraint(a, pltpu.VMEM) for a in results])


def solution(mesh):
    return jax.shard_map(
        functools.partial(body, mesh.shape["gx"], mesh.shape["gy"]),
        mesh=mesh,
        in_specs=(
            P(None, "gx", "gy", None),
            P(None, "gx", "gy", None),
            P("gx", "gy", None),
            P("gx", "gy", None),
            P("gx", "gy", None),
        ),
        out_specs=(P(None, "gx", "gy", None), P("gx", "gy", None), P("gx", "gy", None)),
        check_vma=False,
    )
```
